128 devices in a mesh: span: 32 (over x, z, y_lo), ctx: 4 (over y_hi, core).
Axes of the slice: x: 4, y: 4 (y_hi: 2, y_lo: 2; y = y_hi * 2 + y_lo), z: 4, core: 2. Of those that a mesh axis runs over, the one named last changes fastest.
Arguments:
- queries: bfloat16 [16384, 3072], P(('span', 'ctx')), may hold values from -64 to 64
- keys: bfloat16 [16384, 512], P(('span', 'ctx')), may hold values from -16 to 16
- values: bfloat16 [16384, 512], P(('span', 'ctx')), may hold values from -6 to 6
- temps: float32 [8, 24], replicated, may hold values from 0.5 to 2
- levels: int32 [32], replicated, may hold values from 0 to 7
- ctx_list: int32 [32, 4], replicated, may hold values from -1 to 30, as said below
- counts: int32 [32], replicated, may hold values from 256 to 512
Outputs:
- attended: bfloat16 [16384, 3072], P(('span', 'ctx'))
The draws below stay inside these ranges and needn't reach their ends.
Inputs may be any that keep to these rules, and one draw needn't show every extreme that they name: `ctx_list`: slot 0 of span c's list is c - 1 (-1 for span 0). Slot 1, when used, is span 0. The other slots hold distinct spans below c - 1, used slots first, then -1. The list of span 32 - 1 has no -1.
All inputs are finite; a program needn't handle non-finite values.
Results may differ from the reference program's by a relative error of at most 0.0041.
Values may be sent and summed in bfloat16 or wider, within the bound.
A program may use at most 128 MiB of HBM per device.

```python
import math
import jax
import jax.numpy as jnp
from jax import lax

HQ = 24
KVH = 4
HD = 128
CTXN = 4
LEVELS = 8
SPANS = 32
TOK_SPAN = 512
ROWS = 16384


def base_keys(key):
    raw = jax.random.normal(jax.random.fold_in(key, 11), (ROWS, KVH * HD), jnp.float32)
    return jnp.clip(raw, -6.0, 6.0)


def draw_keys(key, part):
    keys_now = base_keys(key)
    return keys_now.astype(jnp.bfloat16)


def draw_queries(key, part):
    raw = jax.random.normal(jax.random.fold_in(key, 12), (ROWS, HQ * HD), jnp.float32)
    queries_now = jnp.clip(raw, -6.0, 6.0)
    return queries_now.astype(jnp.bfloat16)


def draw_ctx_list(key, part):
    span_ids = jnp.arange(SPANS, dtype=jnp.int32)
    columns = jnp.arange(SPANS, dtype=jnp.int32)
    noise = jax.random.randint(jax.random.fold_in(key, 21), (SPANS, SPANS), 0, 1 << 16)
    boosted = noise + jnp.where(columns == 0, 1 << 17, 0)[None, :]
    scores = boosted * SPANS + columns[None, :]
    allowed = columns[None, :] < span_ids[:, None] - 1
    scores = jnp.where(allowed, scores, -1)
    picked, unused = lax.top_k(scores, CTXN - 1)
    taken = jax.random.randint(jax.random.fold_in(key, 22), (SPANS,), 0, CTXN)
    taken = jnp.where(span_ids == SPANS - 1, CTXN - 1, taken)
    slots = jnp.arange(CTXN - 1, dtype=jnp.int32)
    valid = (picked >= 0) & (slots[None, :] < taken[:, None])
    others = jnp.where(valid, picked % SPANS, -1)
    first = jnp.where(span_ids >= 1, span_ids - 1, -1)
    return jnp.concatenate([first[:, None], others], axis=1).astype(jnp.int32)


def draw_counts(key, part):
    drawn = jax.random.randint(jax.random.fold_in(key, 31), (SPANS,), TOK_SPAN // 2, TOK_SPAN + 1)
    span_ids = jnp.arange(SPANS, dtype=jnp.int32)
    drawn = jnp.where(span_ids == 0, TOK_SPAN, drawn)
    drawn = jnp.where(span_ids == 1, TOK_SPAN // 2, drawn)
    return drawn.astype(jnp.int32)


def set_ends(values, own_key, least, high):
    longest = values.shape.index(max(values.shape))
    spots = []
    for shift in (0, 1):
        where = [jax.random.randint(jax.random.fold_in(own_key, axis), (), 0, length) for axis, length in enumerate(values.shape)]
        where[longest] = (where[longest] + shift) % values.shape[longest]
        spots.append(tuple(where))
    return values.at[spots[0]].set(least).at[spots[1]].set(high)


def level_of(stream_key, shape, split, least, largest):
    def one(axis_at, parts):
        steps = jax.random.uniform(jax.random.fold_in(jax.random.fold_in(stream_key, 6), axis_at), (parts,), jnp.float32, least / len(split), largest / len(split))
        return jnp.repeat(jnp.exp(steps), shape[axis_at] // parts).reshape((-1,) + (1,) * (len(shape) - axis_at - 1))

    gain = one(*split[0])
    for cut in split[1:]:
        gain = gain * one(*cut)
    return gain


def bell_draw(stream_key, extent, width, limit, cuts=(), kind=jnp.bfloat16):
    values = jax.random.normal(stream_key, extent, jnp.float32) * width
    if len(cuts) > 0:
        values = level_of(stream_key, extent, cuts, -0.22, 0.18) * values
    return jnp.clip(values, min=-limit, max=limit).astype(kind)


def setup_inputs(seed: int = 0) -> dict:
    streams_of = jax.random.split(jax.random.key(seed), 8)
    queries = draw_queries(jax.random.fold_in(streams_of[7], 71), 0)
    keys = draw_keys(jax.random.fold_in(streams_of[7], 71), 0)
    values = bell_draw(streams_of[2], (ROWS, KVH * HD), 1.0, 6.0, ((0, 128),))
    temps = jnp.clip(jnp.exp(jax.random.uniform(streams_of[3], (LEVELS, HQ), jnp.float32, math.log(0.5), math.log(2.0))), 0.5, 2.0)
    levels = set_ends(jax.random.randint(streams_of[4], (SPANS,), 0, LEVELS), jax.random.fold_in(streams_of[4], 1), 0, LEVELS - 1).astype(jnp.int32)
    ctx_list = draw_ctx_list(jax.random.fold_in(streams_of[7], 71), 0)
    counts = draw_counts(jax.random.fold_in(streams_of[7], 71), 0)
    return {"queries": queries, "keys": keys, "values": values, "temps": temps, "levels": levels, "ctx_list": ctx_list, "counts": counts}


def reference(queries, keys, values, temps, levels, ctx_list, counts):
    group_size = HQ // KVH
    key_rows = keys.reshape(SPANS, TOK_SPAN, KVH * HD)
    value_rows = values.reshape(SPANS, TOK_SPAN, KVH * HD)
    query_rows = queries.reshape(SPANS, TOK_SPAN, HQ, HD)
    positions = jnp.arange(TOK_SPAN, dtype=jnp.int32)

    def one_span(span_id):
        span_ids = jnp.concatenate([span_id[None], ctx_list[span_id]]).astype(jnp.int32)
        safe_ids = jnp.maximum(span_ids, 0)
        mask = (span_ids[:, None] >= 0) & (positions[None, :] < counts[safe_ids][:, None])
        mask = mask.reshape(-1)
        all_keys = key_rows[safe_ids].reshape(-1, KVH * HD).astype(jnp.float32)
        all_values = value_rows[safe_ids].reshape(-1, KVH * HD).astype(jnp.float32)
        query_here = query_rows[span_id].astype(jnp.float32)
        scale = temps[levels[span_id]] / math.sqrt(HD)
        pieces = []
        for kv_head in range(KVH):
            lower = kv_head * group_size
            query_group = query_here[:, lower:lower + group_size]
            key_group = all_keys[:, kv_head * HD:(kv_head + 1) * HD]
            value_group = all_values[:, kv_head * HD:(kv_head + 1) * HD]
            scores = jnp.einsum('tgd,kd->gtk', query_group, key_group) * scale[lower:lower + group_size][:, None, None]
            scores = jnp.where(mask[None, None, :], scores, -1e+30)
            highest = lax.optimization_barrier(jnp.max(scores, axis=-1, keepdims=True))
            weights = jnp.where(mask[None, None, :], jnp.exp(scores - highest), 0.0)
            totals = lax.optimization_barrier(jnp.sum(weights, axis=-1))
            rounded = lax.optimization_barrier(weights.astype(jnp.bfloat16)).astype(jnp.float32)
            summed = jnp.einsum('gtk,kd->tgd', rounded, value_group)
            pieces.append(summed / jnp.transpose(totals)[:, :, None])
        joined = jnp.concatenate(pieces, axis=1)
        return joined.reshape(TOK_SPAN, HQ * HD).astype(jnp.bfloat16)
    result = lax.map(one_span, jnp.arange(SPANS, dtype=jnp.int32))
    return result.reshape(ROWS, HQ * HD)
```

```python
import functools
import math

import jax
import jax.numpy as jnp
from jax import lax
from jax.experimental import pallas as pl
from jax.experimental.pallas import tpu as pltpu
from jax.sharding import PartitionSpec as P

HQ = 24
KVH = 4
HD = 128
GROUP = HQ // KVH
WIDE = GROUP * HD
TOK = 512
PIECE = 128
SLOTS = 5
MESH = pl.DeviceIdType.MESH


def place():
    s = lax.axis_index("span")
    t = lax.axis_index("ctx")
    x = lax.div(s, 8)
    z = lax.rem(lax.div(s, 2), 4)
    y = lax.div(t, 2) * 2 + lax.rem(s, 2)
    core = lax.rem(t, 2)
    return s, t, x, z, y, core


def device(x, z, y, core):
    return ((x * 4 + z) * 2 + lax.rem(y, 2), lax.div(y, 2) * 2 + core)


def greet(targets):
    barrier = pltpu.get_barrier_semaphore()
    for target in targets:
        pl.semaphore_signal(barrier, inc=1, device_id=target, device_id_type=MESH)
    pl.semaphore_wait(barrier, len(targets))


def column_mates(x, z, y, core):
    flat = y * 2 + core
    mates = []
    for step in range(1, 8):
        other = lax.rem(flat + step, 8)
        mates.append(device(x, z, lax.div(other, 2), lax.rem(other, 2)))
    return mates


def gather_kernel(q_ref, k_ref, v_ref, g_ref, qa_ref, col_send, col_recv, ring_send, ring_recv, pair_send, pair_recv):
    s, t, x, z, y, core = place()
    yl = lax.rem(s, 2)

    def along(axis, step):
        moved = lax.rem((x if axis == 0 else z) + step + 4, 4)
        return device(moved, z, y, core) if axis == 0 else device(x, moved, y, core)

    greet(column_mates(x, z, y, core) + [along(axis, step) for axis in (0, 1) for step in (1, -1)])

    column = x * 4 + z
    sources = [k_ref, v_ref, q_ref]

    def landing(kind, parity, piece):
        rows = pl.ds(pl.multiple_of(piece * PIECE, PIECE), PIECE)
        if kind == 2:
            return qa_ref.at[rows, :]
        return g_ref.at[parity, kind, column, rows, :]

    def column_copy(kind, head):
        width = WIDE if kind == 2 else HD
        return pltpu.make_async_remote_copy(
            src_ref=sources[kind].at[:, pl.ds(head * width, width)],
            dst_ref=landing(kind, yl, t),
            send_sem=col_send.at[kind, head],
            recv_sem=col_recv.at[kind, t],
            device_id=device(x, z, head, yl),
            device_id_type=MESH,
        )

    def own_copy(kind, head):
        width = WIDE if kind == 2 else HD
        return pltpu.make_async_copy(
            sources[kind].at[:, pl.ds(head * width, width)], landing(kind, yl, t), col_recv.at[kind, t]
        )

    for kind in range(3):
        for head in range(KVH):
            mine = (y == head) & (core == yl)

            @pl.when(mine)
            def _():
                own_copy(kind, head).start()

            @pl.when(jnp.logical_not(mine))
            def _():
                column_copy(kind, head).start()

    def await_column(kind):
        for piece in range(4):
            spot = landing(kind, core, piece)
            pltpu.make_async_copy(spot, spot, col_recv.at[kind, piece]).wait()

    started = []

    def block_of(kv, da, db):
        first, second = (x, z) if kv == 0 else (z, x)
        first = lax.rem(first + da + 4, 4)
        second = lax.rem(second + db + 4, 4)
        return first * 4 + second if kv == 0 else second * 4 + first

    def rows_of(half):
        return pl.ds(0, TOK) if half is None else pl.ds(half * (TOK // 2), TOK // 2)

    def send(kv, da, db, half, leg, step):
        axis = leg if kv == 0 else 1 - leg
        block = block_of(kv, da, db)
        spot = g_ref.at[core, kv, block, rows_of(half), :]
        copy = pltpu.make_async_remote_copy(
            src_ref=spot,
            dst_ref=spot,
            send_sem=ring_send.at[len(started)],
            recv_sem=ring_recv.at[kv, block, half or 0],
            device_id=along(axis, step),
            device_id_type=MESH,
        )
        copy.start()
        started.append(copy)

    def arrive(kv, da, db, half):
        block = block_of(kv, da, db)
        spot = g_ref.at[core, kv, block, rows_of(half), :]
        pltpu.make_async_copy(spot, spot, ring_recv.at[kv, block, half or 0]).wait()

    paired = []

    def pair(kv, da, db):
        block = block_of(kv, da, db)
        spot = g_ref.at[core, kv, block]
        copy = pltpu.make_async_remote_copy(
            src_ref=spot,
            dst_ref=spot,
            send_sem=pair_send.at[len(paired)],
            recv_sem=pair_recv.at[kv, block],
            device_id=device(x, z, y, 1 - core),
            device_id_type=MESH,
        )
        copy.start()
        paired.append(copy)

    for kv in (0, 1):
        await_column(kv)
        for step in (1, -1):
            send(kv, 0, 0, None, 0, step)
    for kv in (0, 1):
        for step in (1, -1):
            send(kv, 0, 0, None, 1, step)
        pair(kv, 0, 0)
    for kv in (0, 1):
        arrive(kv, -1, 0, None)
        send(kv, -1, 0, 0, 0, 1)
        arrive(kv, 1, 0, None)
        send(kv, 1, 0, 1, 0, -1)
    for kv in (0, 1):
        for da in (-1, 1):
            for step in (1, -1):
                send(kv, da, 0, None, 1, step)
            pair(kv, da, 0)
    for kv in (0, 1):
        arrive(kv, 2, 0, 0)
        arrive(kv, 2, 0, 1)
        for step in (1, -1):
            send(kv, 2, 0, None, 1, step)
        pair(kv, 2, 0)
    for da in (0, -1, 1, 2):
        for kv in (0, 1):
            arrive(kv, da, -1, None)
            send(kv, da, -1, 0, 1, 1)
            pair(kv, da, -1)
            arrive(kv, da, 1, None)
            send(kv, da, 1, 1, 1, -1)
            pair(kv, da, 1)
    for da in (0, -1, 1, 2):
        for kv in (0, 1):
            arrive(kv, da, 2, 0)
            arrive(kv, da, 2, 1)
            pair(kv, da, 2)
    for kv in (0, 1):
        for block in range(16):
            spot = g_ref.at[1 - core, kv, block]
            pltpu.make_async_copy(spot, spot, pair_recv.at[kv, block]).wait()
    await_column(2)
    for kind in range(3):
        for head in range(KVH):

            @pl.when(jnp.logical_not((y == head) & (core == yl)))
            def _():
                column_copy(kind, head).wait_send()

    for copy in started + paired:
        copy.wait_send()


def gather(queries, keys, values):
    anywhere = pl.BlockSpec(memory_space=pl.ANY)
    return pl.pallas_call(
        gather_kernel,
        out_shape=(
            jax.ShapeDtypeStruct((2, 2, 16, TOK, HD), jnp.bfloat16),
            jax.ShapeDtypeStruct((TOK, WIDE), jnp.bfloat16),
        ),
        in_specs=[anywhere] * 3,
        out_specs=(anywhere, anywhere),
        scratch_shapes=[
            pltpu.SemaphoreType.DMA((3, 4)),
            pltpu.SemaphoreType.DMA((3, 4)),
            pltpu.SemaphoreType.DMA((40,)),
            pltpu.SemaphoreType.DMA((2, 16, 2)),
            pltpu.SemaphoreType.DMA((32,)),
            pltpu.SemaphoreType.DMA((2, 16)),
        ],
        compiler_params=pltpu.CompilerParams(collective_id=0, has_side_effects=True),
        name="gather_blocks",
    )(queries, keys, values)


def attend_kernel(temps, levels, ctx_list, counts, q_ref, g_ref, o_ref, kraw, vraw, kx, vx, sems):
    s, t, x, z, y, core = place()
    span = (x * 4 + z) * 2 + core
    ids = [span] + [ctx_list[span, j] for j in range(SLOTS - 1)]

    def fetch(slot):
        source = jnp.where(ids[slot] >= 0, ids[slot], span)
        parity, column = lax.rem(source, 2), lax.div(source, 2)
        return (
            pltpu.make_async_copy(g_ref.at[parity, 0, column], kraw.at[slot], sems.at[0, slot]),
            pltpu.make_async_copy(g_ref.at[parity, 1, column], vraw.at[slot], sems.at[1, slot]),
        )

    for slot in range(SLOTS):
        for copy in fetch(slot):
            copy.start()
    position = lax.broadcasted_iota(jnp.int32, (TOK, HD), 0)
    for slot in range(SLOTS):
        for copy in fetch(slot):
            copy.wait()
        source = jnp.where(ids[slot] >= 0, ids[slot], span)
        length = counts[source]
        rows = pl.ds(slot * TOK, TOK)
        key = kraw[slot].astype(jnp.float32)
        kx[rows, :] = jnp.where(position < length, key, key[0:1, :]).astype(jnp.bfloat16)
        used = jnp.where(ids[slot] >= 0, length, 0)
        value = vraw[slot].astype(jnp.float32)
        vx[rows, 0:HD] = jnp.where(position < used, value, 0.0).astype(jnp.bfloat16)
        vx[rows, HD : 2 * HD] = jnp.where(position < used, 1.0, 0.0).astype(jnp.bfloat16)
    level = levels[span]
    chunk = 256
    for head in range(GROUP):
        scale = temps[level, y * GROUP + head] * (math.log2(math.e) / math.sqrt(HD))
        for part in range(TOK // chunk):
            rows = pl.ds(part * chunk, chunk)
            cols = pl.ds(head * HD, HD)
            scores = lax.dot_general(
                q_ref[rows, cols], kx[...], (((1,), (1,)), ((), ())), preferred_element_type=jnp.float32
            )
            top = jnp.max(scores, axis=1, keepdims=True)
            weight = jnp.exp2((scores - top) * scale).astype(jnp.bfloat16)
            both = jnp.dot(weight, vx[...], preferred_element_type=jnp.float32)
            o_ref[rows, cols] = (both[:, 0:HD] / both[:, HD : 2 * HD]).astype(jnp.bfloat16)


def attend(temps, levels, ctx_list, counts, q_all, blocks):
    smem = pl.BlockSpec(memory_space=pltpu.SMEM)
    vmem = pl.BlockSpec(memory_space=pltpu.VMEM)
    return pl.pallas_call(
        attend_kernel,
        out_shape=jax.ShapeDtypeStruct((TOK, WIDE), jnp.bfloat16),
        in_specs=[smem] * 4 + [vmem, pl.BlockSpec(memory_space=pl.ANY)],
        out_specs=vmem,
        scratch_shapes=[
            pltpu.VMEM((SLOTS, TOK, HD), jnp.bfloat16),
            pltpu.VMEM((SLOTS, TOK, HD), jnp.bfloat16),
            pltpu.VMEM((SLOTS * TOK, HD), jnp.bfloat16),
            pltpu.VMEM((SLOTS * TOK, 2 * HD), jnp.bfloat16),
            pltpu.SemaphoreType.DMA((2, SLOTS)),
        ],
        compiler_params=pltpu.CompilerParams(vmem_limit_bytes=56 * 1024 * 1024),
        name="attend",
    )(temps, levels, ctx_list, counts, q_all, blocks)


def spread_kernel(o_ref, out_ref, send_sem, recv_sem):
    s, t, x, z, y, core = place()
    greet(column_mates(x, z, y, core))

    def owner(piece):
        return device(x, z, core + 2 * (piece // 2), piece % 2)

    def columns(head):
        return pl.ds(pl.multiple_of(head * WIDE, WIDE), WIDE)

    def remote(piece):
        return pltpu.make_async_remote_copy(
            src_ref=o_ref.at[pl.ds(piece * PIECE, PIECE), :],
            dst_ref=out_ref.at[:, columns(y)],
            send_sem=send_sem.at[piece],
            recv_sem=recv_sem.at[y],
            device_id=owner(piece),
            device_id_type=MESH,
        )

    def mine(piece):
        return (t == piece) & (lax.rem(s, 2) == core)

    for piece in range(4):

        @pl.when(mine(piece))
        def _():
            pltpu.make_async_copy(
                o_ref.at[pl.ds(piece * PIECE, PIECE), :], out_ref.at[:, columns(y)], recv_sem.at[y]
            ).start()

        @pl.when(jnp.logical_not(mine(piece)))
        def _():
            remote(piece).start()

    for head in range(KVH):
        spot = out_ref.at[:, columns(head)]
        pltpu.make_async_copy(spot, spot, recv_sem.at[head]).wait()
    for piece in range(4):

        @pl.when(jnp.logical_not(mine(piece)))
        def _():
            remote(piece).wait_send()


def spread(outputs):
    anywhere = pl.BlockSpec(memory_space=pl.ANY)
    return pl.pallas_call(
        spread_kernel,
        out_shape=jax.ShapeDtypeStruct((PIECE, HQ * HD), jnp.bfloat16),
        in_specs=[anywhere],
        out_specs=anywhere,
        scratch_shapes=[pltpu.SemaphoreType.DMA((4,)), pltpu.SemaphoreType.DMA((4,))],
        compiler_params=pltpu.CompilerParams(collective_id=1, has_side_effects=True),
        name="spread_outputs",
    )(outputs)


def per_device(queries, keys, values, temps, levels, ctx_list, counts):
    blocks, q_all = gather(queries, keys, values)
    outputs = attend(temps, levels, ctx_list, counts, q_all, blocks)
    return spread(outputs)


def solution(mesh):
    return jax.shard_map(
        per_device,
        mesh=mesh,
        in_specs=(
            P(("span", "ctx"), None),
            P(("span", "ctx"), None),
            P(("span", "ctx"), None),
            P(),
            P(),
            P(),
            P(),
        ),
        out_specs=P(("span", "ctx"), None),
        check_vma=False,
    )
```

```python
import functools
import math

import jax
import jax.numpy as jnp
from jax import lax
from jax.experimental import pallas as pl
from jax.experimental.pallas import tpu as pltpu
from jax.sharding import PartitionSpec as P

HQ = 24
KVH = 4
HD = 128
GROUP = HQ // KVH
WIDE = GROUP * HD
TOK = 512
PIECE = 128
SLOTS = 5
EARLY = 2
CHUNK = 256
MESH = pl.DeviceIdType.MESH


def place():
    s = lax.axis_index("span")
    t = lax.axis_index("ctx")
    x = lax.div(s, 8)
    z = lax.rem(lax.div(s, 2), 4)
    y = lax.div(t, 2) * 2 + lax.rem(s, 2)
    core = lax.rem(t, 2)
    return s, t, x, z, y, core


def device(x, z, y, core):
    return ((x * 4 + z) * 2 + lax.rem(y, 2), lax.div(y, 2) * 2 + core)


def greet(targets):
    barrier = pltpu.get_barrier_semaphore()
    for target in targets:
        pl.semaphore_signal(barrier, inc=1, device_id=target, device_id_type=MESH)
    pl.semaphore_wait(barrier, len(targets))


def column_mates(x, z, y, core):
    flat = y * 2 + core
    mates = []
    for step in range(1, 8):
        other = lax.rem(flat + step, 8)
        mates.append(device(x, z, lax.div(other, 2), lax.rem(other, 2)))
    return mates


def fused_kernel(
    temps, levels, ctx_t, counts, q_ref, k_ref, v_ref, out_ref,
    g_ref, qa_ref, kx, vx, acc_ref, top_ref, o_ref,
    col_send, col_recv, ring_send, ring_recv, pair_send, pair_recv, out_send, out_recv,
):
    s, t, x, z, y, core = place()
    yl = lax.rem(s, 2)
    column = x * 4 + z
    span = column * 2 + core

    def along(axis, step):
        moved = lax.rem((x if axis == 0 else z) + step + 4, 4)
        return device(moved, z, y, core) if axis == 0 else device(x, moved, y, core)

    greet(column_mates(x, z, y, core) + [along(axis, step) for axis in (0, 1) for step in (1, -1)])

    sources = [k_ref, v_ref, q_ref]

    def landing(kind, parity, piece):
        rows = pl.ds(pl.multiple_of(piece * PIECE, PIECE), PIECE)
        if kind == 2:
            return qa_ref.at[rows, :]
        return g_ref.at[parity, kind, column, rows, :]

    def column_copy(kind, head):
        width = WIDE if kind == 2 else HD
        return pltpu.make_async_remote_copy(
            src_ref=sources[kind].at[:, pl.ds(head * width, width)],
            dst_ref=landing(kind, yl, t),
            send_sem=col_send.at[kind, head],
            recv_sem=col_recv.at[kind, t],
            device_id=device(x, z, head, yl),
            device_id_type=MESH,
        )

    def own_copy(kind, head):
        width = WIDE if kind == 2 else HD
        return pltpu.make_async_copy(
            sources[kind].at[:, pl.ds(head * width, width)], landing(kind, yl, t), col_recv.at[kind, t]
        )

    for kind in range(3):
        for head in range(KVH):
            mine = (y == head) & (core == yl)

            @pl.when(mine)
            def _():
                own_copy(kind, head).start()

            @pl.when(jnp.logical_not(mine))
            def _():
                column_copy(kind, head).start()

    def await_column(kind):
        for piece in range(4):
            spot = landing(kind, core, piece)
            pltpu.make_async_copy(spot, spot, col_recv.at[kind, piece]).wait()

    started = []

    def block_of(kv, da, db):
        first, second = (x, z) if kv == 0 else (z, x)
        first = lax.rem(first + da + 4, 4)
        second = lax.rem(second + db + 4, 4)
        return first * 4 + second if kv == 0 else second * 4 + first

    def rows_of(half):
        return pl.ds(0, TOK) if half is None else pl.ds(half * (TOK // 2), TOK // 2)

    def send(kv, da, db, half, leg, step):
        axis = leg if kv == 0 else 1 - leg
        block = block_of(kv, da, db)
        spot = g_ref.at[core, kv, block, rows_of(half), :]
        copy = pltpu.make_async_remote_copy(
            src_ref=spot,
            dst_ref=spot,
            send_sem=ring_send.at[len(started)],
            recv_sem=ring_recv.at[kv, block, half or 0],
            device_id=along(axis, step),
            device_id_type=MESH,
        )
        copy.start()
        started.append(copy)

    def arrive(kv, da, db, half):
        block = block_of(kv, da, db)
        spot = g_ref.at[core, kv, block, rows_of(half), :]
        pltpu.make_async_copy(spot, spot, ring_recv.at[kv, block, half or 0]).wait()

    paired = []

    def pair(kv, da, db):
        block = block_of(kv, da, db)
        spot = g_ref.at[core, kv, block]
        copy = pltpu.make_async_remote_copy(
            src_ref=spot,
            dst_ref=spot,
            send_sem=pair_send.at[len(paired)],
            recv_sem=pair_recv.at[kv, block],
            device_id=device(x, z, y, 1 - core),
            device_id_type=MESH,
        )
        copy.start()
        paired.append(copy)

    def await_pair(kv, block):
        spot = g_ref.at[1 - core, kv, block]
        pltpu.make_async_copy(spot, spot, pair_recv.at[kv, block]).wait()

    position = lax.broadcasted_iota(jnp.int32, (TOK, HD), 0)

    def prepare(slot, source, used):
        parity, place_of = lax.rem(source, 2), lax.div(source, 2)
        length = counts[source]
        rows = pl.ds(slot * TOK, TOK)
        key = g_ref[parity, 0, place_of].astype(jnp.float32)
        kx[rows, :] = jnp.where(position < length, key, key[0:1, :]).astype(jnp.bfloat16)
        limit = jnp.where(used, length, 0)
        value = g_ref[parity, 1, place_of].astype(jnp.float32)
        vx[rows, 0:HD] = jnp.where(position < limit, value, 0.0).astype(jnp.bfloat16)
        vx[rows, HD : 2 * HD] = jnp.where(position < limit, 1.0, 0.0).astype(jnp.bfloat16)

    level = levels[span]

    def scale_of(head):
        return temps[level, y * GROUP + head] * (math.log2(math.e) / math.sqrt(HD))

    def scores_of(head, part, low, high):
        return lax.dot_general(
            qa_ref[pl.ds(part * CHUNK, CHUNK), pl.ds(head * HD, HD)],
            kx[pl.ds(low * TOK, (high - low) * TOK), :],
            (((1,), (1,)), ((), ())),
            preferred_element_type=jnp.float32,
        )

    def early(piece):
        head, part = piece // (TOK // CHUNK), piece % (TOK // CHUNK)
        rows = pl.ds(part * CHUNK, CHUNK)
        scores = scores_of(head, part, 0, EARLY)
        top = jnp.max(scores, axis=1, keepdims=True)
        weight = jnp.exp2((scores - top) * scale_of(head)).astype(jnp.bfloat16)
        top_ref[head, rows, :] = jnp.broadcast_to(top, (CHUNK, HD))
        acc_ref[head, rows, :] = jnp.dot(
            weight, vx[pl.ds(0, EARLY * TOK), :], preferred_element_type=jnp.float32
        )

    def late(head, part):
        rows = pl.ds(part * CHUNK, CHUNK)
        scale = scale_of(head)
        scores = scores_of(head, part, EARLY, SLOTS)
        before = top_ref[head, rows, 0:1]
        top = jnp.maximum(before, jnp.max(scores, axis=1, keepdims=True))
        weight = jnp.exp2((scores - top) * scale).astype(jnp.bfloat16)
        both = jnp.dot(
            weight, vx[pl.ds(EARLY * TOK, (SLOTS - EARLY) * TOK), :], preferred_element_type=jnp.float32
        )
        both = both + acc_ref[head, rows, :] * jnp.exp2((before - top) * scale)
        o_ref[rows, pl.ds(head * HD, HD)] = (both[:, 0:HD] / both[:, HD : 2 * HD]).astype(jnp.bfloat16)

    for kv in (0, 1):
        await_column(kv)
        for step in (1, -1):
            send(kv, 0, 0, None, 0, step)
    for kv in (0, 1):
        for step in (1, -1):
            send(kv, 0, 0, None, 1, step)
        pair(kv, 0, 0)
    for kv in (0, 1):
        arrive(kv, -1, 0, None)
        send(kv, -1, 0, 0, 0, 1)
        arrive(kv, 1, 0, None)
        send(kv, 1, 0, 1, 0, -1)
    for kv in (0, 1):
        for da in (-1, 1):
            for step in (1, -1):
                send(kv, da, 0, None, 1, step)
            pair(kv, da, 0)
    for kv in (0, 1):
        arrive(kv, 2, 0, 0)
        arrive(kv, 2, 0, 1)
        for step in (1, -1):
            send(kv, 2, 0, None, 1, step)
        pair(kv, 2, 0)
    prepare(0, span, True)
    await_column(2)

    def hop(kv, da):
        arrive(kv, da, -1, None)
        send(kv, da, -1, 0, 1, 1)
        pair(kv, da, -1)
        arrive(kv, da, 1, None)
        send(kv, da, 1, 1, 1, -1)
        pair(kv, da, 1)

    def last_hop(kv, da):
        arrive(kv, da, 2, 0)
        arrive(kv, da, 2, 1)
        pair(kv, da, 2)

    for da in (0, -1):
        for kv in (0, 1):
            hop(kv, da)
    near = lax.rem(column + core + 15, 16)
    for kv in (0, 1):
        await_pair(kv, near)
    prepare(1, lax.rem(span + 31, 32), span > 0)
    steps = [functools.partial(hop, kv, da) for da in (1, 2) for kv in (0, 1)]
    steps += [functools.partial(last_hop, kv, da) for da in (0, -1, 1, 2) for kv in (0, 1)]
    for piece, step in enumerate(steps):
        step()
        early(piece)
    for kv in (0, 1):
        for block in range(16):

            @pl.when(block != near)
            def _():
                await_pair(kv, block)

    for slot in range(EARLY, SLOTS):
        listed = ctx_t[slot - 1, span]
        prepare(slot, jnp.where(listed >= 0, listed, span), listed >= 0)

    def out_columns(role, head):
        return pl.ds(pl.multiple_of(role * WIDE + head * HD, HD), HD)

    def out_copy(head, piece):
        return pltpu.make_async_remote_copy(
            src_ref=o_ref.at[pl.ds(piece * PIECE, PIECE), pl.ds(head * HD, HD)],
            dst_ref=out_ref.at[:, out_columns(y, head)],
            send_sem=out_send.at[head, piece],
            recv_sem=out_recv.at[y, head],
            device_id=device(x, z, core + 2 * (piece // 2), piece % 2),
            device_id_type=MESH,
        )

    def kept(piece):
        return (t == piece) & (yl == core)

    def send_out(head):
        for piece in range(4):

            @pl.when(kept(piece))
            def _():
                pltpu.make_async_copy(
                    o_ref.at[pl.ds(piece * PIECE, PIECE), pl.ds(head * HD, HD)],
                    out_ref.at[:, out_columns(y, head)],
                    out_recv.at[y, head],
                ).start()

            @pl.when(jnp.logical_not(kept(piece)))
            def _():
                out_copy(head, piece).start()

    for head in range(GROUP):
        for part in range(TOK // CHUNK):
            late(head, part)
            if head > 0 and part == 0:
                send_out(head - 1)
    for kind in range(3):
        for head in range(KVH):

            @pl.when(jnp.logical_not((y == head) & (core == yl)))
            def _():
                column_copy(kind, head).wait_send()

    for copy in started + paired:
        copy.wait_send()
    send_out(GROUP - 1)
    for role in range(KVH):
        for head in range(GROUP):
            spot = out_ref.at[:, out_columns(role, head)]
            pltpu.make_async_copy(spot, spot, out_recv.at[role, head]).wait()
    for head in range(GROUP):
        for piece in range(4):

            @pl.when(jnp.logical_not(kept(piece)))
            def _():
                out_copy(head, piece).wait_send()


def per_device(queries, keys, values, temps, levels, ctx_list, counts):
    anywhere = pl.BlockSpec(memory_space=pl.ANY)
    smem = pl.BlockSpec(memory_space=pltpu.SMEM)
    dma = pltpu.SemaphoreType.DMA
    return pl.pallas_call(
        fused_kernel,
        out_shape=jax.ShapeDtypeStruct((PIECE, HQ * HD), jnp.bfloat16),
        in_specs=[smem] * 4 + [anywhere] * 3,
        out_specs=anywhere,
        scratch_shapes=[
            pltpu.VMEM((2, 2, 16, TOK, HD), jnp.bfloat16),
            pltpu.VMEM((TOK, WIDE), jnp.bfloat16),
            pltpu.VMEM((SLOTS * TOK, HD), jnp.bfloat16),
            pltpu.VMEM((SLOTS * TOK, 2 * HD), jnp.bfloat16),
            pltpu.VMEM((GROUP, TOK, 2 * HD), jnp.float32),
            pltpu.VMEM((GROUP, TOK, HD), jnp.float32),
            pltpu.VMEM((TOK, WIDE), jnp.bfloat16),
            dma((3, 4)),
            dma((3, 4)),
            dma((40,)),
            dma((2, 16, 2)),
            dma((32,)),
            dma((2, 16)),
            dma((GROUP, 4)),
            dma((KVH, GROUP)),
        ],
        compiler_params=pltpu.CompilerParams(
            collective_id=0, has_side_effects=True, vmem_limit_bytes=56 * 1024 * 1024
        ),
        name="span_attention",
    )(temps, levels, ctx_list.T, counts, queries, keys, values)


def solution(mesh):
    return jax.shard_map(
        per_device,
        mesh=mesh,
        in_specs=(
            P(("span", "ctx"), None),
            P(("span", "ctx"), None),
            P(("span", "ctx"), None),
            P(),
            P(),
            P(),
            P(),
        ),
        out_specs=P(("span", "ctx"), None),
        check_vma=False,
    )
```

```python
import functools
import math

import jax
import jax.numpy as jnp
from jax import lax
from jax.experimental import pallas as pl
from jax.experimental.pallas import tpu as pltpu
from jax.sharding import PartitionSpec as P

HQ = 24
KVH = 4
HD = 128
GROUP = HQ // KVH
WIDE = GROUP * HD
TOK = 512
PIECE = 128
SLOTS = 5
EARLY = 2
CHUNK = 256
MESH = pl.DeviceIdType.MESH


def place():
    s = lax.axis_index("span")
    t = lax.axis_index("ctx")
    x = lax.div(s, 8)
    z = lax.rem(lax.div(s, 2), 4)
    y = lax.div(t, 2) * 2 + lax.rem(s, 2)
    core = lax.rem(t, 2)
    return s, t, x, z, y, core


def device(x, z, y, core):
    return ((x * 4 + z) * 2 + lax.rem(y, 2), lax.div(y, 2) * 2 + core)


def greet(targets):
    barrier = pltpu.get_barrier_semaphore()
    for target in targets:
        pl.semaphore_signal(barrier, inc=1, device_id=target, device_id_type=MESH)
    pl.semaphore_wait(barrier, len(targets))


def column_mates(x, z, y, core):
    flat = y * 2 + core
    mates = []
    for step in range(1, 8):
        other = lax.rem(flat + step, 8)
        mates.append(device(x, z, lax.div(other, 2), lax.rem(other, 2)))
    return mates


def fused_kernel(
    temps, levels, ctx_t, counts, q_ref, k_ref, v_ref, out_ref,
    g_ref, qa_ref, kx, vx, acc_ref, top_ref, o_ref,
    col_send, col_recv, ring_send, ring_recv, pair_send, pair_recv, out_send, out_recv,
):
    s, t, x, z, y, core = place()
    yl = lax.rem(s, 2)
    column = x * 4 + z
    span = column * 2 + core

    def along(axis, step):
        moved = lax.rem((x if axis == 0 else z) + step + 4, 4)
        return device(moved, z, y, core) if axis == 0 else device(x, moved, y, core)

    greet(column_mates(x, z, y, core) + [along(axis, step) for axis in (0, 1) for step in (1, -1)])

    sources = [k_ref, v_ref, q_ref]

    def landing(kind, parity, piece):
        rows = pl.ds(pl.multiple_of(piece * PIECE, PIECE), PIECE)
        if kind == 2:
            return qa_ref.at[rows, :]
        return g_ref.at[parity, kind, column, rows, :]

    def column_copy(kind, head):
        width = WIDE if kind == 2 else HD
        return pltpu.make_async_remote_copy(
            src_ref=sources[kind].at[:, pl.ds(head * width, width)],
            dst_ref=landing(kind, yl, t),
            send_sem=col_send.at[kind, head],
            recv_sem=col_recv.at[kind, t],
            device_id=device(x, z, head, yl),
            device_id_type=MESH,
        )

    def own_copy(kind, head):
        width = WIDE if kind == 2 else HD
        return pltpu.make_async_copy(
            sources[kind].at[:, pl.ds(head * width, width)], landing(kind, yl, t), col_recv.at[kind, t]
        )

    for kind in range(3):
        for head in range(KVH):
            mine = (y == head) & (core == yl)

            @pl.when(mine)
            def _():
                own_copy(kind, head).start()

            @pl.when(jnp.logical_not(mine))
            def _():
                column_copy(kind, head).start()

    def await_piece(kind, piece):
        spot = landing(kind, core, piece)
        pltpu.make_async_copy(spot, spot, col_recv.at[kind, piece]).wait()

    close = jnp.where(y - core == 2, 1, 0)
    halves = (close, 1 - close)

    started = []

    def block_of(kv, da, db):
        first, second = (x, z) if kv == 0 else (z, x)
        first = lax.rem(first + da + 4, 4)
        second = lax.rem(second + db + 4, 4)
        return first * 4 + second if kv == 0 else second * 4 + first

    def rows_of(half):
        return pl.ds(pl.multiple_of(halves[half] * (TOK // 2), TOK // 2), TOK // 2)

    def send(kv, da, db, half, leg, step):
        axis = leg if kv == 0 else 1 - leg
        block = block_of(kv, da, db)
        spot = g_ref.at[core, kv, block, rows_of(half), :]
        copy = pltpu.make_async_remote_copy(
            src_ref=spot,
            dst_ref=spot,
            send_sem=ring_send.at[len(started)],
            recv_sem=ring_recv.at[kv, block, half],
            device_id=along(axis, step),
            device_id_type=MESH,
        )
        copy.start()
        started.append(copy)

    def arrive(kv, da, db, half):
        block = block_of(kv, da, db)
        spot = g_ref.at[core, kv, block, rows_of(half), :]
        pltpu.make_async_copy(spot, spot, ring_recv.at[kv, block, half]).wait()

    paired = []

    def pair(kv, da, db):
        block = block_of(kv, da, db)
        spot = g_ref.at[core, kv, block]
        copy = pltpu.make_async_remote_copy(
            src_ref=spot,
            dst_ref=spot,
            send_sem=pair_send.at[len(paired)],
            recv_sem=pair_recv.at[kv, block],
            device_id=device(x, z, y, 1 - core),
            device_id_type=MESH,
        )
        copy.start()
        paired.append(copy)

    def await_pair(kv, block):
        spot = g_ref.at[1 - core, kv, block]
        pltpu.make_async_copy(spot, spot, pair_recv.at[kv, block]).wait()

    position = lax.broadcasted_iota(jnp.int32, (TOK, HD), 0)

    def prepare(slot, source, used):
        parity, place_of = lax.rem(source, 2), lax.div(source, 2)
        length = counts[source]
        rows = pl.ds(slot * TOK, TOK)
        key = g_ref[parity, 0, place_of].astype(jnp.float32)
        kx[rows, :] = jnp.where(position < length, key, key[0:1, :]).astype(jnp.bfloat16)
        limit = jnp.where(used, length, 0)
        value = g_ref[parity, 1, place_of].astype(jnp.float32)
        vx[rows, 0:HD] = jnp.where(position < limit, value, 0.0).astype(jnp.bfloat16)
        vx[rows, HD : 2 * HD] = jnp.where(position < limit, 1.0, 0.0).astype(jnp.bfloat16)

    level = levels[span]

    def scale_of(head):
        return temps[level, y * GROUP + head] * (math.log2(math.e) / math.sqrt(HD))

    def scores_of(head, part, low, high):
        return lax.dot_general(
            qa_ref[pl.ds(part * CHUNK, CHUNK), pl.ds(head * HD, HD)],
            kx[pl.ds(low * TOK, (high - low) * TOK), :],
            (((1,), (1,)), ((), ())),
            preferred_element_type=jnp.float32,
        )

    def early(piece):
        head, part = piece // (TOK // CHUNK), piece % (TOK // CHUNK)
        rows = pl.ds(part * CHUNK, CHUNK)
        scores = scores_of(head, part, 0, EARLY)
        top = jnp.max(scores, axis=1, keepdims=True)
        weight = jnp.exp2((scores - top) * scale_of(head)).astype(jnp.bfloat16)
        top_ref[head, rows, :] = jnp.broadcast_to(top, (CHUNK, HD))
        acc_ref[head, rows, :] = jnp.dot(
            weight, vx[pl.ds(0, EARLY * TOK), :], preferred_element_type=jnp.float32
        )

    def late(head, part):
        rows = pl.ds(part * CHUNK, CHUNK)
        scale = scale_of(head)
        scores = scores_of(head, part, EARLY, SLOTS)
        before = top_ref[head, rows, 0:1]
        top = jnp.maximum(before, jnp.max(scores, axis=1, keepdims=True))
        weight = jnp.exp2((scores - top) * scale).astype(jnp.bfloat16)
        both = jnp.dot(
            weight, vx[pl.ds(EARLY * TOK, (SLOTS - EARLY) * TOK), :], preferred_element_type=jnp.float32
        )
        both = both + acc_ref[head, rows, :] * jnp.exp2((before - top) * scale)
        o_ref[rows, pl.ds(head * HD, HD)] = (both[:, 0:HD] / both[:, HD : 2 * HD]).astype(jnp.bfloat16)

    for kv in (0, 1):
        for half in (0, 1):
            for row in (0, 1):
                await_piece(kv, 2 * halves[half] + row)
            for leg in (0, 1):
                for step in (1, -1):
                    send(kv, 0, 0, half, leg, step)
        pair(kv, 0, 0)
    for kv in (0, 1):
        for half in (0, 1):
            for da in (-1, 1):
                arrive(kv, da, 0, half)
                if half == (da + 1) // 2:
                    send(kv, da, 0, half, 0, -da)
                for step in (1, -1):
                    send(kv, da, 0, half, 1, step)
        pair(kv, -1, 0)
        pair(kv, 1, 0)
    for kv in (0, 1):
        for half in (0, 1):
            arrive(kv, 2, 0, half)
            for step in (1, -1):
                send(kv, 2, 0, half, 1, step)
        pair(kv, 2, 0)
    prepare(0, span, True)
    for piece in range(4):
        await_piece(2, piece)

    def hop(kv, da):
        for half in (0, 1):
            for db in (-1, 1):
                arrive(kv, da, db, half)
                if half == (db + 1) // 2:
                    send(kv, da, db, half, 1, -db)
        pair(kv, da, -1)
        pair(kv, da, 1)

    def last_hop(kv, da):
        arrive(kv, da, 2, 0)
        arrive(kv, da, 2, 1)
        pair(kv, da, 2)

    for da in (0, -1):
        for kv in (0, 1):
            hop(kv, da)
    near = lax.rem(column + core + 15, 16)
    for kv in (0, 1):
        await_pair(kv, near)
    prepare(1, lax.rem(span + 31, 32), span > 0)
    steps = [functools.partial(hop, kv, da) for da in (1, 2) for kv in (0, 1)]
    steps += [functools.partial(last_hop, kv, da) for da in (0, -1, 1, 2) for kv in (0, 1)]
    for piece, step in enumerate(steps):
        step()
        early(piece)
    for kv in (0, 1):
        for block in range(16):

            @pl.when(block != near)
            def _():
                await_pair(kv, block)

    for slot in range(EARLY, SLOTS):
        listed = ctx_t[slot - 1, span]
        prepare(slot, jnp.where(listed >= 0, listed, span), listed >= 0)

    def out_columns(role, head):
        return pl.ds(pl.multiple_of(role * WIDE + head * HD, HD), HD)

    def out_copy(head, piece):
        return pltpu.make_async_remote_copy(
            src_ref=o_ref.at[pl.ds(piece * PIECE, PIECE), pl.ds(head * HD, HD)],
            dst_ref=out_ref.at[:, out_columns(y, head)],
            send_sem=out_send.at[head, piece],
            recv_sem=out_recv.at[y, head],
            device_id=device(x, z, core + 2 * (piece // 2), piece % 2),
            device_id_type=MESH,
        )

    def kept(piece):
        return (t == piece) & (yl == core)

    def send_out(head):
        for piece in range(4):

            @pl.when(kept(piece))
            def _():
                pltpu.make_async_copy(
                    o_ref.at[pl.ds(piece * PIECE, PIECE), pl.ds(head * HD, HD)],
                    out_ref.at[:, out_columns(y, head)],
                    out_recv.at[y, head],
                ).start()

            @pl.when(jnp.logical_not(kept(piece)))
            def _():
                out_copy(head, piece).start()

    for head in range(GROUP):
        for part in range(TOK // CHUNK):
            late(head, part)
            if head > 0 and part == 0:
                send_out(head - 1)
    for kind in range(3):
        for head in range(KVH):

            @pl.when(jnp.logical_not((y == head) & (core == yl)))
            def _():
                column_copy(kind, head).wait_send()

    for copy in started + paired:
        copy.wait_send()
    send_out(GROUP - 1)
    for role in range(KVH):
        for head in range(GROUP):
            spot = out_ref.at[:, out_columns(role, head)]
            pltpu.make_async_copy(spot, spot, out_recv.at[role, head]).wait()
    for head in range(GROUP):
        for piece in range(4):

            @pl.when(jnp.logical_not(kept(piece)))
            def _():
                out_copy(head, piece).wait_send()


def per_device(queries, keys, values, temps, levels, ctx_list, counts):
    anywhere = pl.BlockSpec(memory_space=pl.ANY)
    smem = pl.BlockSpec(memory_space=pltpu.SMEM)
    dma = pltpu.SemaphoreType.DMA
    return pl.pallas_call(
        fused_kernel,
        out_shape=jax.ShapeDtypeStruct((PIECE, HQ * HD), jnp.bfloat16),
        in_specs=[smem] * 4 + [anywhere] * 3,
        out_specs=anywhere,
        scratch_shapes=[
            pltpu.VMEM((2, 2, 16, TOK, HD), jnp.bfloat16),
            pltpu.VMEM((TOK, WIDE), jnp.bfloat16),
            pltpu.VMEM((SLOTS * TOK, HD), jnp.bfloat16),
            pltpu.VMEM((SLOTS * TOK, 2 * HD), jnp.bfloat16),
            pltpu.VMEM((GROUP, TOK, 2 * HD), jnp.float32),
            pltpu.VMEM((GROUP, TOK, HD), jnp.float32),
            pltpu.VMEM((TOK, WIDE), jnp.bfloat16),
            dma((3, 4)),
            dma((3, 4)),
            dma((60,)),
            dma((2, 16, 2)),
            dma((32,)),
            dma((2, 16)),
            dma((GROUP, 4)),
            dma((KVH, GROUP)),
        ],
        compiler_params=pltpu.CompilerParams(
            collective_id=0, has_side_effects=True, vmem_limit_bytes=56 * 1024 * 1024
        ),
        name="span_attention",
    )(temps, levels, ctx_list.T, counts, queries, keys, values)


def solution(mesh):
    return jax.shard_map(
        per_device,
        mesh=mesh,
        in_specs=(
            P(("span", "ctx"), None),
            P(("span", "ctx"), None),
            P(("span", "ctx"), None),
            P(),
            P(),
            P(),
            P(),
        ),
        out_specs=P(("span", "ctx"), None),
        check_vma=False,
    )
```

```python
import functools
import math

import jax
import jax.numpy as jnp
from jax import lax
from jax.experimental import pallas as pl
from jax.experimental.pallas import tpu as pltpu
from jax.sharding import PartitionSpec as P

HQ = 24
KVH = 4
HD = 128
GROUP = HQ // KVH
WIDE = GROUP * HD
TOK = 512
PIECE = 128
SLOTS = 5
EARLY = 2
CHUNK = 256
PARTS = TOK // CHUNK
PIECES = GROUP * PARTS
SPREAD = (1,) * 12
MESH = pl.DeviceIdType.MESH


def place():
    s = lax.axis_index("span")
    t = lax.axis_index("ctx")
    x = lax.div(s, 8)
    z = lax.rem(lax.div(s, 2), 4)
    y = lax.div(t, 2) * 2 + lax.rem(s, 2)
    core = lax.rem(t, 2)
    return s, t, x, z, y, core


def device(x, z, y, core):
    return ((x * 4 + z) * 2 + lax.rem(y, 2), lax.div(y, 2) * 2 + core)


def greet(targets):
    barrier = pltpu.get_barrier_semaphore()
    for target in targets:
        pl.semaphore_signal(barrier, inc=1, device_id=target, device_id_type=MESH)
    pl.semaphore_wait(barrier, len(targets))


def column_mates(x, z, y, core):
    flat = y * 2 + core
    mates = []
    for step in range(1, 8):
        other = lax.rem(flat + step, 8)
        mates.append(device(x, z, lax.div(other, 2), lax.rem(other, 2)))
    return mates


def fused_kernel(
    temps, levels, ctx_t, counts, q_ref, k_ref, v_ref, out_ref,
    g_ref, qa_ref, kx, vx, acc_ref, top_ref, o_ref,
    col_send, col_recv, ring_send, ring_recv, pair_send, pair_recv, out_send, out_recv,
):
    s, t, x, z, y, core = place()
    yl = lax.rem(s, 2)
    column = x * 4 + z
    span = column * 2 + core

    def along(axis, step):
        moved = lax.rem((x if axis == 0 else z) + step + 4, 4)
        return device(moved, z, y, core) if axis == 0 else device(x, moved, y, core)

    greet(column_mates(x, z, y, core) + [along(axis, step) for axis in (0, 1) for step in (1, -1)])

    sources = [k_ref, v_ref, q_ref]

    def landing(kind, parity, piece):
        rows = pl.ds(pl.multiple_of(piece * PIECE, PIECE), PIECE)
        if kind == 2:
            return qa_ref.at[rows, :]
        return g_ref.at[parity, kind, column, rows, :]

    def column_copy(kind, head):
        width = WIDE if kind == 2 else HD
        return pltpu.make_async_remote_copy(
            src_ref=sources[kind].at[:, pl.ds(head * width, width)],
            dst_ref=landing(kind, yl, t),
            send_sem=col_send.at[kind, head],
            recv_sem=col_recv.at[kind, t],
            device_id=device(x, z, head, yl),
            device_id_type=MESH,
        )

    def own_copy(kind, head):
        width = WIDE if kind == 2 else HD
        return pltpu.make_async_copy(
            sources[kind].at[:, pl.ds(head * width, width)], landing(kind, yl, t), col_recv.at[kind, t]
        )

    for kind in range(3):
        for head in range(KVH):
            mine = (y == head) & (core == yl)

            @pl.when(mine)
            def _():
                own_copy(kind, head).start()

            @pl.when(jnp.logical_not(mine))
            def _():
                column_copy(kind, head).start()

    def await_piece(kind, piece):
        spot = landing(kind, core, piece)
        pltpu.make_async_copy(spot, spot, col_recv.at[kind, piece]).wait()

    close = jnp.where(y - core == 2, 1, 0)
    halves = (close, 1 - close)

    started = []

    def block_of(kv, da, db):
        first, second = (x, z) if kv == 0 else (z, x)
        first = lax.rem(first + da + 4, 4)
        second = lax.rem(second + db + 4, 4)
        return first * 4 + second if kv == 0 else second * 4 + first

    def rows_of(half):
        return pl.ds(pl.multiple_of(halves[half] * (TOK // 2), TOK // 2), TOK // 2)

    def send(kv, da, db, half, leg, step):
        axis = leg if kv == 0 else 1 - leg
        block = block_of(kv, da, db)
        spot = g_ref.at[core, kv, block, rows_of(half), :]
        copy = pltpu.make_async_remote_copy(
            src_ref=spot,
            dst_ref=spot,
            send_sem=ring_send.at[len(started)],
            recv_sem=ring_recv.at[kv, block, half],
            device_id=along(axis, step),
            device_id_type=MESH,
        )
        copy.start()
        started.append(copy)

    def arrive(kv, da, db, half):
        block = block_of(kv, da, db)
        spot = g_ref.at[core, kv, block, rows_of(half), :]
        pltpu.make_async_copy(spot, spot, ring_recv.at[kv, block, half]).wait()

    paired = []

    def pair(kv, da, db):
        block = block_of(kv, da, db)
        spot = g_ref.at[core, kv, block]
        copy = pltpu.make_async_remote_copy(
            src_ref=spot,
            dst_ref=spot,
            send_sem=pair_send.at[len(paired)],
            recv_sem=pair_recv.at[kv, block],
            device_id=device(x, z, y, 1 - core),
            device_id_type=MESH,
        )
        copy.start()
        paired.append(copy)

    def await_pair(kv, block):
        spot = g_ref.at[1 - core, kv, block]
        pltpu.make_async_copy(spot, spot, pair_recv.at[kv, block]).wait()

    position = lax.broadcasted_iota(jnp.int32, (TOK, HD), 0)

    def prepare(slot, source, used):
        parity, place_of = lax.rem(source, 2), lax.div(source, 2)
        length = counts[source]
        rows = pl.ds(slot * TOK, TOK)
        key = g_ref[parity, 0, place_of].astype(jnp.float32)
        kx[rows, :] = jnp.where(position < length, key, key[0:1, :]).astype(jnp.bfloat16)
        limit = jnp.where(used, length, 0)
        value = g_ref[parity, 1, place_of].astype(jnp.float32)
        vx[rows, 0:HD] = jnp.where(position < limit, value, 0.0).astype(jnp.bfloat16)
        vx[rows, HD : 2 * HD] = jnp.where(position < limit, 1.0, 0.0).astype(jnp.bfloat16)

    level = levels[span]

    def scale_of(head):
        return temps[level, y * GROUP + head] * (math.log2(math.e) / math.sqrt(HD))

    def scores_of(head, part, low, high):
        return lax.dot_general(
            qa_ref[pl.ds(part * CHUNK, CHUNK), pl.ds(head * HD, HD)],
            kx[pl.ds(low * TOK, (high - low) * TOK), :],
            (((1,), (1,)), ((), ())),
            preferred_element_type=jnp.float32,
        )

    def early_scores(piece):
        return scores_of(piece // PARTS, piece % PARTS, 0, EARLY)

    def early(piece, scores):
        head, part = piece // PARTS, piece % PARTS
        rows = pl.ds(part * CHUNK, CHUNK)
        top = jnp.max(scores, axis=1, keepdims=True)
        weight = jnp.exp2((scores - top) * scale_of(head)).astype(jnp.bfloat16)
        top_ref[head, rows, :] = jnp.broadcast_to(top, (CHUNK, HD))
        acc_ref[head, rows, :] = jnp.dot(
            weight, vx[pl.ds(0, EARLY * TOK), :], preferred_element_type=jnp.float32
        )

    def late_scores(piece):
        return scores_of(piece // PARTS, piece % PARTS, EARLY, SLOTS)

    def late(piece, scores):
        head, part = piece // PARTS, piece % PARTS
        rows = pl.ds(part * CHUNK, CHUNK)
        scale = scale_of(head)
        before = top_ref[head, rows, 0:1]
        top = jnp.maximum(before, jnp.max(scores, axis=1, keepdims=True))
        weight = jnp.exp2((scores - top) * scale).astype(jnp.bfloat16)
        both = jnp.dot(
            weight, vx[pl.ds(EARLY * TOK, (SLOTS - EARLY) * TOK), :], preferred_element_type=jnp.float32
        )
        both = both + acc_ref[head, rows, :] * jnp.exp2((before - top) * scale)
        o_ref[rows, pl.ds(head * HD, HD)] = (both[:, 0:HD] / both[:, HD : 2 * HD]).astype(jnp.bfloat16)

    for kv in (0, 1):
        for half in (0, 1):
            for row in (0, 1):
                await_piece(kv, 2 * halves[half] + row)
            for leg in (0, 1):
                for step in (1, -1):
                    send(kv, 0, 0, half, leg, step)
        pair(kv, 0, 0)
    for kv in (0, 1):
        for half in (0, 1):
            for da in (-1, 1):
                arrive(kv, da, 0, half)
                if half == (da + 1) // 2:
                    send(kv, da, 0, half, 0, -da)
                for step in (1, -1):
                    send(kv, da, 0, half, 1, step)
        pair(kv, -1, 0)
        pair(kv, 1, 0)
    for kv in (0, 1):
        for half in (0, 1):
            arrive(kv, 2, 0, half)
            for step in (1, -1):
                send(kv, 2, 0, half, 1, step)
        pair(kv, 2, 0)
    prepare(0, span, True)
    for piece in range(4):
        await_piece(2, piece)

    def hop(kv, da):
        for half in (0, 1):
            for db in (-1, 1):
                arrive(kv, da, db, half)
                if half == (db + 1) // 2:
                    send(kv, da, db, half, 1, -db)
        pair(kv, da, -1)
        pair(kv, da, 1)

    def last_hop(kv, da):
        arrive(kv, da, 2, 0)
        arrive(kv, da, 2, 1)
        pair(kv, da, 2)

    for da in (0, -1):
        for kv in (0, 1):
            hop(kv, da)
    near = lax.rem(column + core + 15, 16)
    for kv in (0, 1):
        await_pair(kv, near)
    prepare(1, lax.rem(span + 31, 32), span > 0)
    steps = [functools.partial(hop, kv, da) for da in (1, 2) for kv in (0, 1)]
    steps += [functools.partial(last_hop, kv, da) for da in (0, -1, 1, 2) for kv in (0, 1)]
    piece = 0
    scores = early_scores(0)
    for step, share in zip(steps, SPREAD):
        step()
        for _ in range(share):
            ahead = early_scores(piece + 1) if piece + 1 < PIECES else None
            early(piece, scores)
            piece, scores = piece + 1, ahead
    for kv in (0, 1):
        for block in range(16):

            @pl.when(block != near)
            def _():
                await_pair(kv, block)

    for slot in range(EARLY, SLOTS):
        listed = ctx_t[slot - 1, span]
        prepare(slot, jnp.where(listed >= 0, listed, span), listed >= 0)

    def out_columns(role, head):
        return pl.ds(pl.multiple_of(role * WIDE + head * HD, HD), HD)

    def out_copy(head, piece):
        return pltpu.make_async_remote_copy(
            src_ref=o_ref.at[pl.ds(piece * PIECE, PIECE), pl.ds(head * HD, HD)],
            dst_ref=out_ref.at[:, out_columns(y, head)],
            send_sem=out_send.at[head, piece],
            recv_sem=out_recv.at[y, head],
            device_id=device(x, z, core + 2 * (piece // 2), piece % 2),
            device_id_type=MESH,
        )

    def kept(piece):
        return (t == piece) & (yl == core)

    def send_out(head, part):
        for piece in (2 * part, 2 * part + 1):

            @pl.when(kept(piece))
            def _():
                pltpu.make_async_copy(
                    o_ref.at[pl.ds(piece * PIECE, PIECE), pl.ds(head * HD, HD)],
                    out_ref.at[:, out_columns(y, head)],
                    out_recv.at[y, head],
                ).start()

            @pl.when(jnp.logical_not(kept(piece)))
            def _():
                out_copy(head, piece).start()

    scores = late_scores(0)
    for piece in range(PIECES):
        ahead = late_scores(piece + 1) if piece + 1 < PIECES else None
        late(piece, scores)
        scores = ahead
        if piece > 0:
            send_out((piece - 1) // PARTS, (piece - 1) % PARTS)
    for kind in range(3):
        for head in range(KVH):

            @pl.when(jnp.logical_not((y == head) & (core == yl)))
            def _():
                column_copy(kind, head).wait_send()

    for copy in started + paired:
        copy.wait_send()
    send_out(GROUP - 1, PARTS - 1)
    for role in range(KVH):
        for head in range(GROUP):
            spot = out_ref.at[:, out_columns(role, head)]
            pltpu.make_async_copy(spot, spot, out_recv.at[role, head]).wait()
    for head in range(GROUP):
        for piece in range(4):

            @pl.when(jnp.logical_not(kept(piece)))
            def _():
                out_copy(head, piece).wait_send()


def per_device(queries, keys, values, temps, levels, ctx_list, counts):
    anywhere = pl.BlockSpec(memory_space=pl.ANY)
    smem = pl.BlockSpec(memory_space=pltpu.SMEM)
    dma = pltpu.SemaphoreType.DMA
    return pl.pallas_call(
        fused_kernel,
        out_shape=jax.ShapeDtypeStruct((PIECE, HQ * HD), jnp.bfloat16),
        in_specs=[smem] * 4 + [anywhere] * 3,
        out_specs=anywhere,
        scratch_shapes=[
            pltpu.VMEM((2, 2, 16, TOK, HD), jnp.bfloat16),
            pltpu.VMEM((TOK, WIDE), jnp.bfloat16),
            pltpu.VMEM((SLOTS * TOK, HD), jnp.bfloat16),
            pltpu.VMEM((SLOTS * TOK, 2 * HD), jnp.bfloat16),
            pltpu.VMEM((GROUP, TOK, 2 * HD), jnp.float32),
            pltpu.VMEM((GROUP, TOK, HD), jnp.float32),
            pltpu.VMEM((TOK, WIDE), jnp.bfloat16),
            dma((3, 4)),
            dma((3, 4)),
            dma((60,)),
            dma((2, 16, 2)),
            dma((32,)),
            dma((2, 16)),
            dma((GROUP, 4)),
            dma((KVH, GROUP)),
        ],
        compiler_params=pltpu.CompilerParams(
            collective_id=0, has_side_effects=True, vmem_limit_bytes=56 * 1024 * 1024
        ),
        name="span_attention",
    )(temps, levels, ctx_list.T, counts, queries, keys, values)


def solution(mesh):
    return jax.shard_map(
        per_device,
        mesh=mesh,
        in_specs=(
            P(("span", "ctx"), None),
            P(("span", "ctx"), None),
            P(("span", "ctx"), None),
            P(),
            P(),
            P(),
            P(),
        ),
        out_specs=P(("span", "ctx"), None),
        check_vma=False,
    )
```

```python
import functools
import math

import jax
import jax.numpy as jnp
from jax import lax
from jax.experimental import pallas as pl
from jax.experimental.pallas import tpu as pltpu
from jax.sharding import PartitionSpec as P

HQ = 24
KVH = 4
HD = 128
GROUP = HQ // KVH
WIDE = GROUP * HD
TOK = 512
PIECE = 128
SLOTS = 5
EARLY = 2
CHUNK = 512
PARTS = TOK // CHUNK
PIECES = GROUP * PARTS
SPREAD = (1,) * GROUP + (0,) * 6
MESH = pl.DeviceIdType.MESH


def place():
    s = lax.axis_index("span")
    t = lax.axis_index("ctx")
    x = lax.div(s, 8)
    z = lax.rem(lax.div(s, 2), 4)
    y = lax.div(t, 2) * 2 + lax.rem(s, 2)
    core = lax.rem(t, 2)
    return s, t, x, z, y, core


def device(x, z, y, core):
    return ((x * 4 + z) * 2 + lax.rem(y, 2), lax.div(y, 2) * 2 + core)


def greet(targets):
    barrier = pltpu.get_barrier_semaphore()
    for target in targets:
        pl.semaphore_signal(barrier, inc=1, device_id=target, device_id_type=MESH)
    pl.semaphore_wait(barrier, len(targets))


def column_mates(x, z, y, core):
    flat = y * 2 + core
    mates = []
    for step in range(1, 8):
        other = lax.rem(flat + step, 8)
        mates.append(device(x, z, lax.div(other, 2), lax.rem(other, 2)))
    return mates


def fused_kernel(
    temps, levels, ctx_t, counts, q_ref, k_ref, v_ref, out_ref,
    g_ref, qa_ref, kx, vx, acc_ref, top_ref, o_ref,
    col_send, col_recv, ring_send, ring_recv, pair_send, pair_recv, out_send, out_recv,
):
    s, t, x, z, y, core = place()
    yl = lax.rem(s, 2)
    column = x * 4 + z
    span = column * 2 + core

    def along(axis, step):
        moved = lax.rem((x if axis == 0 else z) + step + 4, 4)
        return device(moved, z, y, core) if axis == 0 else device(x, moved, y, core)

    greet(column_mates(x, z, y, core) + [along(axis, step) for axis in (0, 1) for step in (1, -1)])

    sources = [k_ref, v_ref, q_ref]

    def landing(kind, parity, piece):
        rows = pl.ds(pl.multiple_of(piece * PIECE, PIECE), PIECE)
        if kind == 2:
            return qa_ref.at[rows, :]
        return g_ref.at[parity, kind, column, rows, :]

    def column_copy(kind, head):
        width = WIDE if kind == 2 else HD
        return pltpu.make_async_remote_copy(
            src_ref=sources[kind].at[:, pl.ds(head * width, width)],
            dst_ref=landing(kind, yl, t),
            send_sem=col_send.at[kind, head],
            recv_sem=col_recv.at[kind, t],
            device_id=device(x, z, head, yl),
            device_id_type=MESH,
        )

    def own_copy(kind, head):
        width = WIDE if kind == 2 else HD
        return pltpu.make_async_copy(
            sources[kind].at[:, pl.ds(head * width, width)], landing(kind, yl, t), col_recv.at[kind, t]
        )

    def scatter(kind):
        for head in range(KVH):
            mine = (y == head) & (core == yl)

            @pl.when(mine)
            def _():
                own_copy(kind, head).start()

            @pl.when(jnp.logical_not(mine))
            def _():
                column_copy(kind, head).start()

    scatter(0)
    scatter(1)

    def await_piece(kind, piece):
        spot = landing(kind, core, piece)
        pltpu.make_async_copy(spot, spot, col_recv.at[kind, piece]).wait()

    close = jnp.where(y - core == 2, 1, 0)
    halves = (close, 1 - close)

    started = []

    def block_of(kv, da, db):
        first, second = (x, z) if kv == 0 else (z, x)
        first = lax.rem(first + da + 4, 4)
        second = lax.rem(second + db + 4, 4)
        return first * 4 + second if kv == 0 else second * 4 + first

    def rows_of(half):
        return pl.ds(pl.multiple_of(halves[half] * (TOK // 2), TOK // 2), TOK // 2)

    def send(kv, da, db, half, leg, step):
        axis = leg if kv == 0 else 1 - leg
        block = block_of(kv, da, db)
        spot = g_ref.at[core, kv, block, rows_of(half), :]
        copy = pltpu.make_async_remote_copy(
            src_ref=spot,
            dst_ref=spot,
            send_sem=ring_send.at[len(started)],
            recv_sem=ring_recv.at[kv, block, half],
            device_id=along(axis, step),
            device_id_type=MESH,
        )
        copy.start()
        started.append(copy)

    def arrive(kv, da, db, half):
        block = block_of(kv, da, db)
        spot = g_ref.at[core, kv, block, rows_of(half), :]
        pltpu.make_async_copy(spot, spot, ring_recv.at[kv, block, half]).wait()

    paired = []

    def pair(kv, da, db):
        block = block_of(kv, da, db)
        spot = g_ref.at[core, kv, block]
        copy = pltpu.make_async_remote_copy(
            src_ref=spot,
            dst_ref=spot,
            send_sem=pair_send.at[len(paired)],
            recv_sem=pair_recv.at[kv, block],
            device_id=device(x, z, y, 1 - core),
            device_id_type=MESH,
        )
        copy.start()
        paired.append(copy)

    def await_pair(kv, block):
        spot = g_ref.at[1 - core, kv, block]
        pltpu.make_async_copy(spot, spot, pair_recv.at[kv, block]).wait()

    position = lax.broadcasted_iota(jnp.int32, (TOK, HD), 0)

    def prepare(slot, source, used):
        parity, place_of = lax.rem(source, 2), lax.div(source, 2)
        length = counts[source]
        rows = pl.ds(slot * TOK, TOK)
        key = g_ref[parity, 0, place_of].astype(jnp.float32)
        kx[rows, :] = jnp.where(position < length, key, key[0:1, :]).astype(jnp.bfloat16)
        limit = jnp.where(used, length, 0)
        value = g_ref[parity, 1, place_of].astype(jnp.float32)
        vx[rows, 0:HD] = jnp.where(position < limit, value, 0.0).astype(jnp.bfloat16)
        vx[rows, HD : 2 * HD] = jnp.where(position < limit, 1.0, 0.0).astype(jnp.bfloat16)

    level = levels[span]

    def scale_of(head):
        return temps[level, y * GROUP + head] * (math.log2(math.e) / math.sqrt(HD))

    def scores_of(head, part, low, high):
        return lax.dot_general(
            qa_ref[pl.ds(part * CHUNK, CHUNK), pl.ds(head * HD, HD)],
            kx[pl.ds(low * TOK, (high - low) * TOK), :],
            (((1,), (1,)), ((), ())),
            preferred_element_type=jnp.float32,
        )

    def early_scores(piece):
        return scores_of(piece // PARTS, piece % PARTS, 0, EARLY)

    def early(piece, scores):
        head, part = piece // PARTS, piece % PARTS
        rows = pl.ds(part * CHUNK, CHUNK)
        top = jnp.max(scores, axis=1, keepdims=True)
        weight = jnp.exp2((scores - top) * scale_of(head)).astype(jnp.bfloat16)
        top_ref[head, rows, :] = jnp.broadcast_to(top, (CHUNK, HD))
        acc_ref[head, rows, :] = jnp.dot(
            weight, vx[pl.ds(0, EARLY * TOK), :], preferred_element_type=jnp.float32
        )

    def late_scores(piece):
        return scores_of(piece // PARTS, piece % PARTS, EARLY, SLOTS)

    def late(piece, scores):
        head, part = piece // PARTS, piece % PARTS
        rows = pl.ds(part * CHUNK, CHUNK)
        scale = scale_of(head)
        before = top_ref[head, rows, 0:1]
        top = jnp.maximum(before, jnp.max(scores, axis=1, keepdims=True))
        weight = jnp.exp2((scores - top) * scale).astype(jnp.bfloat16)
        both = jnp.dot(
            weight, vx[pl.ds(EARLY * TOK, (SLOTS - EARLY) * TOK), :], preferred_element_type=jnp.float32
        )
        both = both + acc_ref[head, rows, :] * jnp.exp2((before - top) * scale)
        o_ref[rows, pl.ds(head * HD, HD)] = (both[:, 0:HD] / both[:, HD : 2 * HD]).astype(jnp.bfloat16)

    for kv in (0, 1):
        for half in (0, 1):
            for row in (0, 1):
                await_piece(kv, 2 * halves[half] + row)
            for leg in (0, 1):
                for step in (1, -1):
                    send(kv, 0, 0, half, leg, step)
        pair(kv, 0, 0)
    scatter(2)

    def hop(kv, da):
        for half in (0, 1):
            for db in (-1, 1):
                arrive(kv, da, db, half)
                if half == (db + 1) // 2:
                    send(kv, da, db, half, 1, -db)
        pair(kv, da, -1)
        pair(kv, da, 1)

    for kv in (0, 1):
        for half in (0, 1):
            for da in (-1, 1):
                arrive(kv, da, 0, half)
                if half == (da + 1) // 2:
                    send(kv, da, 0, half, 0, -da)
        hop(kv, 0)
    for kv in (0, 1):
        for half in (0, 1):
            for da in (-1, 1):
                for step in (1, -1):
                    send(kv, da, 0, half, 1, step)
        pair(kv, -1, 0)
        pair(kv, 1, 0)
    for kv in (0, 1):
        for half in (0, 1):
            arrive(kv, 2, 0, half)
            for step in (1, -1):
                send(kv, 2, 0, half, 1, step)
        pair(kv, 2, 0)
    prepare(0, span, True)
    for piece in range(4):
        await_piece(2, piece)

    def last_hop(kv, da):
        arrive(kv, da, 2, 0)
        arrive(kv, da, 2, 1)
        pair(kv, da, 2)

    for kv in (0, 1):
        hop(kv, -1)
    near = lax.rem(column + core + 15, 16)
    for kv in (0, 1):
        await_pair(kv, near)
    prepare(1, lax.rem(span + 31, 32), span > 0)
    steps = [functools.partial(hop, kv, da) for da in (1, 2) for kv in (0, 1)]
    steps += [functools.partial(last_hop, kv, da) for da in (0, -1, 1, 2) for kv in (0, 1)]
    piece = 0
    scores = early_scores(0)
    for step, share in zip(steps, SPREAD):
        step()
        for _ in range(share):
            ahead = early_scores(piece + 1) if piece + 1 < PIECES else None
            early(piece, scores)
            piece, scores = piece + 1, ahead
    for kv in (0, 1):
        for block in range(16):

            @pl.when(block != near)
            def _():
                await_pair(kv, block)

    for slot in range(EARLY, SLOTS):
        listed = ctx_t[slot - 1, span]
        prepare(slot, jnp.where(listed >= 0, listed, span), listed >= 0)

    def out_columns(role, head):
        return pl.ds(pl.multiple_of(role * WIDE + head * HD, HD), HD)

    def out_copy(head, piece):
        return pltpu.make_async_remote_copy(
            src_ref=o_ref.at[pl.ds(piece * PIECE, PIECE), pl.ds(head * HD, HD)],
            dst_ref=out_ref.at[:, out_columns(y, head)],
            send_sem=out_send.at[head, piece],
            recv_sem=out_recv.at[y, head],
            device_id=device(x, z, core + 2 * (piece // 2), piece % 2),
            device_id_type=MESH,
        )

    def kept(piece):
        return (t == piece) & (yl == core)

    def send_out(head, part):
        for piece in range(part * 4 // PARTS, (part + 1) * 4 // PARTS):

            @pl.when(kept(piece))
            def _():
                pltpu.make_async_copy(
                    o_ref.at[pl.ds(piece * PIECE, PIECE), pl.ds(head * HD, HD)],
                    out_ref.at[:, out_columns(y, head)],
                    out_recv.at[y, head],
                ).start()

            @pl.when(jnp.logical_not(kept(piece)))
            def _():
                out_copy(head, piece).start()

    scores = late_scores(0)
    for piece in range(PIECES):
        ahead = late_scores(piece + 1) if piece + 1 < PIECES else None
        late(piece, scores)
        scores = ahead
        if piece > 0:
            send_out((piece - 1) // PARTS, (piece - 1) % PARTS)
    for kind in range(3):
        for head in range(KVH):

            @pl.when(jnp.logical_not((y == head) & (core == yl)))
            def _():
                column_copy(kind, head).wait_send()

    for copy in started + paired:
        copy.wait_send()
    send_out(GROUP - 1, PARTS - 1)
    for role in range(KVH):
        for head in range(GROUP):
            spot = out_ref.at[:, out_columns(role, head)]
            pltpu.make_async_copy(spot, spot, out_recv.at[role, head]).wait()
    for head in range(GROUP):
        for piece in range(4):

            @pl.when(jnp.logical_not(kept(piece)))
            def _():
                out_copy(head, piece).wait_send()


def per_device(queries, keys, values, temps, levels, ctx_list, counts):
    anywhere = pl.BlockSpec(memory_space=pl.ANY)
    smem = pl.BlockSpec(memory_space=pltpu.SMEM)
    dma = pltpu.SemaphoreType.DMA
    return pl.pallas_call(
        fused_kernel,
        out_shape=jax.ShapeDtypeStruct((PIECE, HQ * HD), jnp.bfloat16),
        in_specs=[smem] * 4 + [anywhere] * 3,
        out_specs=anywhere,
        scratch_shapes=[
            pltpu.VMEM((2, 2, 16, TOK, HD), jnp.bfloat16),
            pltpu.VMEM((TOK, WIDE), jnp.bfloat16),
            pltpu.VMEM((SLOTS * TOK, HD), jnp.bfloat16),
            pltpu.VMEM((SLOTS * TOK, 2 * HD), jnp.bfloat16),
            pltpu.VMEM((GROUP, TOK, 2 * HD), jnp.float32),
            pltpu.VMEM((GROUP, TOK, HD), jnp.float32),
            pltpu.VMEM((TOK, WIDE), jnp.bfloat16),
            dma((3, 4)),
            dma((3, 4)),
            dma((60,)),
            dma((2, 16, 2)),
            dma((32,)),
            dma((2, 16)),
            dma((GROUP, 4)),
            dma((KVH, GROUP)),
        ],
        compiler_params=pltpu.CompilerParams(
            collective_id=0, has_side_effects=True, vmem_limit_bytes=56 * 1024 * 1024
        ),
        name="span_attention",
    )(temps, levels, ctx_list.T, counts, queries, keys, values)


def solution(mesh):
    return jax.shard_map(
        per_device,
        mesh=mesh,
        in_specs=(
            P(("span", "ctx"), None),
            P(("span", "ctx"), None),
            P(("span", "ctx"), None),
            P(),
            P(),
            P(),
            P(),
        ),
        out_specs=P(("span", "ctx"), None),
        check_vma=False,
    )
```

```python
import functools
import math

import jax
import jax.numpy as jnp
from jax import lax
from jax.experimental import pallas as pl
from jax.experimental.pallas import tpu as pltpu
from jax.sharding import PartitionSpec as P

HQ = 24
KVH = 4
HD = 128
GROUP = HQ // KVH
WIDE = GROUP * HD
TOK = 512
PIECE = 128
SLOTS = 5
EARLY = 2
CHUNK = 512
PARTS = TOK // CHUNK
PIECES = GROUP * PARTS
LATE_CHUNK = 256
LATE_PARTS = TOK // LATE_CHUNK
LATE_PIECES = GROUP * LATE_PARTS
SPREAD = (1,) * GROUP + (0,) * 6
MESH = pl.DeviceIdType.MESH


def place():
    s = lax.axis_index("span")
    t = lax.axis_index("ctx")
    x = lax.div(s, 8)
    z = lax.rem(lax.div(s, 2), 4)
    y = lax.div(t, 2) * 2 + lax.rem(s, 2)
    core = lax.rem(t, 2)
    return s, t, x, z, y, core


def device(x, z, y, core):
    return ((x * 4 + z) * 2 + lax.rem(y, 2), lax.div(y, 2) * 2 + core)


def greet(targets):
    barrier = pltpu.get_barrier_semaphore()
    for target in targets:
        pl.semaphore_signal(barrier, inc=1, device_id=target, device_id_type=MESH)
    pl.semaphore_wait(barrier, len(targets))


def column_mates(x, z, y, core):
    flat = y * 2 + core
    mates = []
    for step in range(1, 8):
        other = lax.rem(flat + step, 8)
        mates.append(device(x, z, lax.div(other, 2), lax.rem(other, 2)))
    return mates


def fused_kernel(
    temps, levels, ctx_t, counts, q_ref, k_ref, v_ref, out_ref,
    g_ref, qa_ref, kx, vx, acc_ref, top_ref, o_ref,
    col_send, col_recv, ring_send, ring_recv, pair_send, pair_recv, out_send, out_recv,
):
    s, t, x, z, y, core = place()
    yl = lax.rem(s, 2)
    column = x * 4 + z
    span = column * 2 + core

    def along(axis, step):
        moved = lax.rem((x if axis == 0 else z) + step + 4, 4)
        return device(moved, z, y, core) if axis == 0 else device(x, moved, y, core)

    greet(column_mates(x, z, y, core) + [along(axis, step) for axis in (0, 1) for step in (1, -1)])

    sources = [k_ref, v_ref, q_ref]

    def landing(kind, parity, piece):
        rows = pl.ds(pl.multiple_of(piece * PIECE, PIECE), PIECE)
        if kind == 2:
            return qa_ref.at[rows, :]
        return g_ref.at[parity, kind, column, rows, :]

    def column_copy(kind, head):
        width = WIDE if kind == 2 else HD
        return pltpu.make_async_remote_copy(
            src_ref=sources[kind].at[:, pl.ds(head * width, width)],
            dst_ref=landing(kind, yl, t),
            send_sem=col_send.at[kind, head],
            recv_sem=col_recv.at[kind, t],
            device_id=device(x, z, head, yl),
            device_id_type=MESH,
        )

    def own_copy(kind, head):
        width = WIDE if kind == 2 else HD
        return pltpu.make_async_copy(
            sources[kind].at[:, pl.ds(head * width, width)], landing(kind, yl, t), col_recv.at[kind, t]
        )

    def scatter(kind):
        for head in range(KVH):
            mine = (y == head) & (core == yl)

            @pl.when(mine)
            def _():
                own_copy(kind, head).start()

            @pl.when(jnp.logical_not(mine))
            def _():
                column_copy(kind, head).start()

    scatter(0)
    scatter(1)

    def await_piece(kind, piece):
        spot = landing(kind, core, piece)
        pltpu.make_async_copy(spot, spot, col_recv.at[kind, piece]).wait()

    close = jnp.where(y - core == 2, 1, 0)
    halves = (close, 1 - close)

    started = []

    def block_of(kv, da, db):
        first, second = (x, z) if kv == 0 else (z, x)
        first = lax.rem(first + da + 4, 4)
        second = lax.rem(second + db + 4, 4)
        return first * 4 + second if kv == 0 else second * 4 + first

    def rows_of(half):
        return pl.ds(pl.multiple_of(halves[half] * (TOK // 2), TOK // 2), TOK // 2)

    def send(kv, da, db, half, leg, step):
        axis = leg if kv == 0 else 1 - leg
        block = block_of(kv, da, db)
        spot = g_ref.at[core, kv, block, rows_of(half), :]
        copy = pltpu.make_async_remote_copy(
            src_ref=spot,
            dst_ref=spot,
            send_sem=ring_send.at[len(started)],
            recv_sem=ring_recv.at[kv, block, half],
            device_id=along(axis, step),
            device_id_type=MESH,
        )
        copy.start()
        started.append(copy)

    def arrive(kv, da, db, half):
        block = block_of(kv, da, db)
        spot = g_ref.at[core, kv, block, rows_of(half), :]
        pltpu.make_async_copy(spot, spot, ring_recv.at[kv, block, half]).wait()

    paired = []

    def pair(kv, da, db):
        block = block_of(kv, da, db)
        spot = g_ref.at[core, kv, block]
        copy = pltpu.make_async_remote_copy(
            src_ref=spot,
            dst_ref=spot,
            send_sem=pair_send.at[len(paired)],
            recv_sem=pair_recv.at[kv, block],
            device_id=device(x, z, y, 1 - core),
            device_id_type=MESH,
        )
        copy.start()
        paired.append(copy)

    def await_pair(kv, block):
        spot = g_ref.at[1 - core, kv, block]
        pltpu.make_async_copy(spot, spot, pair_recv.at[kv, block]).wait()

    position = lax.broadcasted_iota(jnp.int32, (TOK, HD), 0)

    def prepare(slot, source, used):
        parity, place_of = lax.rem(source, 2), lax.div(source, 2)
        length = counts[source]
        rows = pl.ds(slot * TOK, TOK)
        key = g_ref[parity, 0, place_of].astype(jnp.float32)
        kx[rows, :] = jnp.where(position < length, key, key[0:1, :]).astype(jnp.bfloat16)
        limit = jnp.where(used, length, 0)
        value = g_ref[parity, 1, place_of].astype(jnp.float32)
        vx[rows, 0:HD] = jnp.where(position < limit, value, 0.0).astype(jnp.bfloat16)
        vx[rows, HD : 2 * HD] = jnp.where(position < limit, 1.0, 0.0).astype(jnp.bfloat16)

    level = levels[span]

    def scale_of(head):
        return temps[level, y * GROUP + head] * (math.log2(math.e) / math.sqrt(HD))

    def scores_of(head, part, low, high, chunk):
        return lax.dot_general(
            qa_ref[pl.ds(part * chunk, chunk), pl.ds(head * HD, HD)],
            kx[pl.ds(low * TOK, (high - low) * TOK), :],
            (((1,), (1,)), ((), ())),
            preferred_element_type=jnp.float32,
        )

    def early_scores(piece):
        return scores_of(piece // PARTS, piece % PARTS, 0, EARLY, CHUNK)

    def early(piece, scores):
        head, part = piece // PARTS, piece % PARTS
        rows = pl.ds(part * CHUNK, CHUNK)
        top = jnp.max(scores, axis=1, keepdims=True)
        weight = jnp.exp2((scores - top) * scale_of(head)).astype(jnp.bfloat16)
        top_ref[head, rows, :] = jnp.broadcast_to(top, (CHUNK, HD))
        acc_ref[head, rows, :] = jnp.dot(
            weight, vx[pl.ds(0, EARLY * TOK), :], preferred_element_type=jnp.float32
        )

    def late_scores(piece):
        return scores_of(piece // LATE_PARTS, piece % LATE_PARTS, EARLY, SLOTS, LATE_CHUNK)

    def late(piece, scores):
        head, part = piece // LATE_PARTS, piece % LATE_PARTS
        rows = pl.ds(part * LATE_CHUNK, LATE_CHUNK)
        scale = scale_of(head)
        before = top_ref[head, rows, 0:1]
        top = jnp.maximum(before, jnp.max(scores, axis=1, keepdims=True))
        weight = jnp.exp2((scores - top) * scale).astype(jnp.bfloat16)
        both = jnp.dot(
            weight, vx[pl.ds(EARLY * TOK, (SLOTS - EARLY) * TOK), :], preferred_element_type=jnp.float32
        )
        both = both + acc_ref[head, rows, :] * jnp.exp2((before - top) * scale)
        o_ref[rows, pl.ds(head * HD, HD)] = (both[:, 0:HD] / both[:, HD : 2 * HD]).astype(jnp.bfloat16)

    for kv in (0, 1):
        for half in (0, 1):
            for row in (0, 1):
                await_piece(kv, 2 * halves[half] + row)
            for leg in (0, 1):
                for step in (1, -1):
                    send(kv, 0, 0, half, leg, step)
        pair(kv, 0, 0)
    scatter(2)

    def hop(kv, da):
        for half in (0, 1):
            for db in (-1, 1):
                arrive(kv, da, db, half)
                if half == (db + 1) // 2:
                    send(kv, da, db, half, 1, -db)
        pair(kv, da, -1)
        pair(kv, da, 1)

    for kv in (0, 1):
        for half in (0, 1):
            for da in (-1, 1):
                arrive(kv, da, 0, half)
                if half == (da + 1) // 2:
                    send(kv, da, 0, half, 0, -da)
        hop(kv, 0)
    for kv in (0, 1):
        for half in (0, 1):
            for da in (-1, 1):
                for step in (1, -1):
                    send(kv, da, 0, half, 1, step)
        pair(kv, -1, 0)
        pair(kv, 1, 0)
    for kv in (0, 1):
        for half in (0, 1):
            arrive(kv, 2, 0, half)
            for step in (1, -1):
                send(kv, 2, 0, half, 1, step)
        pair(kv, 2, 0)
    prepare(0, span, True)
    for piece in range(4):
        await_piece(2, piece)

    def last_hop(kv, da):
        arrive(kv, da, 2, 0)
        arrive(kv, da, 2, 1)
        pair(kv, da, 2)

    for kv in (0, 1):
        hop(kv, -1)
    near = lax.rem(column + core + 15, 16)
    for kv in (0, 1):
        await_pair(kv, near)
    prepare(1, lax.rem(span + 31, 32), span > 0)
    steps = [functools.partial(hop, kv, da) for da in (1, 2) for kv in (0, 1)]
    steps += [functools.partial(last_hop, kv, da) for da in (0, -1, 1, 2) for kv in (0, 1)]
    piece = 0
    scores = early_scores(0)
    for step, share in zip(steps, SPREAD):
        step()
        for _ in range(share):
            ahead = early_scores(piece + 1) if piece + 1 < PIECES else None
            early(piece, scores)
            piece, scores = piece + 1, ahead
    for kv in (0, 1):
        for block in range(16):

            @pl.when(block != near)
            def _():
                await_pair(kv, block)

    for slot in range(EARLY, SLOTS):
        listed = ctx_t[slot - 1, span]
        prepare(slot, jnp.where(listed >= 0, listed, span), listed >= 0)

    def out_columns(role, head):
        return pl.ds(pl.multiple_of(role * WIDE + head * HD, HD), HD)

    def out_copy(head, piece):
        return pltpu.make_async_remote_copy(
            src_ref=o_ref.at[pl.ds(piece * PIECE, PIECE), pl.ds(head * HD, HD)],
            dst_ref=out_ref.at[:, out_columns(y, head)],
            send_sem=out_send.at[head, piece],
            recv_sem=out_recv.at[y, head],
            device_id=device(x, z, core + 2 * (piece // 2), piece % 2),
            device_id_type=MESH,
        )

    def kept(piece):
        return (t == piece) & (yl == core)

    def send_out(head, part):
        for piece in range(part * 4 // LATE_PARTS, (part + 1) * 4 // LATE_PARTS):

            @pl.when(kept(piece))
            def _():
                pltpu.make_async_copy(
                    o_ref.at[pl.ds(piece * PIECE, PIECE), pl.ds(head * HD, HD)],
                    out_ref.at[:, out_columns(y, head)],
                    out_recv.at[y, head],
                ).start()

            @pl.when(jnp.logical_not(kept(piece)))
            def _():
                out_copy(head, piece).start()

    scores = late_scores(0)
    for piece in range(LATE_PIECES):
        ahead = late_scores(piece + 1) if piece + 1 < LATE_PIECES else None
        late(piece, scores)
        scores = ahead
        if piece > 0:
            send_out((piece - 1) // LATE_PARTS, (piece - 1) % LATE_PARTS)
    for kind in range(3):
        for head in range(KVH):

            @pl.when(jnp.logical_not((y == head) & (core == yl)))
            def _():
                column_copy(kind, head).wait_send()

    for copy in started + paired:
        copy.wait_send()
    send_out(GROUP - 1, LATE_PARTS - 1)
    for role in range(KVH):
        for head in range(GROUP):
            spot = out_ref.at[:, out_columns(role, head)]
            pltpu.make_async_copy(spot, spot, out_recv.at[role, head]).wait()
    for head in range(GROUP):
        for piece in range(4):

            @pl.when(jnp.logical_not(kept(piece)))
            def _():
                out_copy(head, piece).wait_send()


def per_device(queries, keys, values, temps, levels, ctx_list, counts):
    anywhere = pl.BlockSpec(memory_space=pl.ANY)
    smem = pl.BlockSpec(memory_space=pltpu.SMEM)
    dma = pltpu.SemaphoreType.DMA
    return pl.pallas_call(
        fused_kernel,
        out_shape=jax.ShapeDtypeStruct((PIECE, HQ * HD), jnp.bfloat16),
        in_specs=[smem] * 4 + [anywhere] * 3,
        out_specs=anywhere,
        scratch_shapes=[
            pltpu.VMEM((2, 2, 16, TOK, HD), jnp.bfloat16),
            pltpu.VMEM((TOK, WIDE), jnp.bfloat16),
            pltpu.VMEM((SLOTS * TOK, HD), jnp.bfloat16),
            pltpu.VMEM((SLOTS * TOK, 2 * HD), jnp.bfloat16),
            pltpu.VMEM((GROUP, TOK, 2 * HD), jnp.float32),
            pltpu.VMEM((GROUP, TOK, HD), jnp.float32),
            pltpu.VMEM((TOK, WIDE), jnp.bfloat16),
            dma((3, 4)),
            dma((3, 4)),
            dma((60,)),
            dma((2, 16, 2)),
            dma((32,)),
            dma((2, 16)),
            dma((GROUP, 4)),
            dma((KVH, GROUP)),
        ],
        compiler_params=pltpu.CompilerParams(
            collective_id=0, has_side_effects=True, vmem_limit_bytes=56 * 1024 * 1024
        ),
        name="span_attention",
    )(temps, levels, ctx_list.T, counts, queries, keys, values)


def solution(mesh):
    return jax.shard_map(
        per_device,
        mesh=mesh,
        in_specs=(
            P(("span", "ctx"), None),
            P(("span", "ctx"), None),
            P(("span", "ctx"), None),
            P(),
            P(),
            P(),
            P(),
        ),
        out_specs=P(("span", "ctx"), None),
        check_vma=False,
    )
```
